32 devices in a mesh: rows: 4 (over y, core), cols: 8 (over z, x).
Axes of the slice: x: 2, y: 2, z: 4, core: 2. Of those that a mesh axis runs over, the one named last changes fastest.
Arguments:
- costs: bfloat16 [4, 8, 24, 256, 256], P('rows', 'cols'), may hold values from -210 to 8
- block_rows: int32 [4, 8, 24], P('rows', 'cols'), may hold values from 0 to 7, as said below
- block_cols: int32 [4, 8, 24], P('rows', 'cols'), may hold values from 0 to 63, as said below
- live: int32 [4, 8], P('rows', 'cols'), may hold values from 16 to 24, as said below
- log_source: float32 [8192], P('rows'), may hold values from -6 to 6
- log_target: float32 [131072], P('cols'), may hold values from -6 to 6
Outputs:
- source_potential: float32 [8192], P('rows')
- target_potential: float32 [131072], P('cols')
The draws below stay inside these ranges and needn't reach their ends.
Inputs may be any that keep to these rules, and one draw needn't show every extreme that they name: `block_rows`: row blocks are local to a device's 8 blocks of source cells. `block_cols`: column blocks are local to a device's 64 blocks of target cells. Every source cell and every target cell lies in some live block. `live`: live counts differ from device to device; some device uses all 24 slots.
All inputs are finite; a program needn't handle non-finite values.
Results may differ from the reference program's by a relative error of at most 0.0003.
Values sent between devices are 32-bit elements; how exact they have to be, the bound alone decides.
A program may use at most 64 MiB of HBM per device.

```python
import jax
import jax.numpy as jnp
from jax import lax

BS = 256
RB_DEV = 8
CB_DEV = 64
EXTRA = 8
ITERS = 3
SLOTS = 24
SRC = 8192
TGT = 131072
N_ROWS = 4
N_COLS = 8


def pair_tables(key):
    base = jax.random.fold_in(key, 7)
    k_rows, k_band, k_live, k_busy = jax.random.split(base, 4)
    must = max(RB_DEV, CB_DEV // N_ROWS)
    share = CB_DEV // N_ROWS
    shape = (N_ROWS, N_COLS, SLOTS)
    slot_ids = jnp.broadcast_to(jnp.arange(SLOTS, dtype=jnp.int32)[None, None, :], shape)
    row_ids = jnp.broadcast_to(jnp.arange(N_ROWS, dtype=jnp.int32)[:, None, None], shape)
    extra_rows = jax.random.randint(k_rows, shape, 0, RB_DEV)
    extra_cols = extra_rows * CB_DEV // RB_DEV + jax.random.randint(k_band, shape, -4, 5)
    extra_cols = jnp.mod(extra_cols, CB_DEV)
    must_rows = jnp.mod(slot_ids, RB_DEV)
    must_cols = jnp.mod(slot_ids, share) * N_ROWS + row_ids
    rows_out = jnp.where(slot_ids < must, must_rows, extra_rows).astype(jnp.int32)
    cols_out = jnp.where(slot_ids < must, must_cols, extra_cols).astype(jnp.int32)
    extra_live = jax.random.randint(k_live, (N_ROWS * N_COLS,), 0, EXTRA + 1)
    busiest = jax.random.randint(k_busy, (), 0, N_ROWS * N_COLS)
    extra_live = jnp.where(jnp.arange(N_ROWS * N_COLS) == busiest, EXTRA, extra_live)
    live_out = (must + extra_live).reshape(N_ROWS, N_COLS).astype(jnp.int32)
    return (rows_out, cols_out, live_out)


def draw_block_rows(key, part):
    return pair_tables(key)[0]


def draw_block_cols(key, part):
    return pair_tables(key)[1]


def draw_live(key, part):
    return pair_tables(key)[2]


def draw_costs(key, part):
    shape = (N_ROWS, N_COLS, SLOTS, BS, BS)
    k_one = jax.random.fold_in(jax.random.fold_in(key, 11), 0)
    values = jnp.clip(2.0 * jax.random.normal(k_one, shape, jnp.float32), -8.0, 8.0)
    return values.astype(jnp.bfloat16)


def shard_levels(stream_key, extent, shards, low, largest):
    factor_of = 1.0
    for dim, shards_of in shards:
        heights = jax.random.uniform(jax.random.fold_in(jax.random.fold_in(stream_key, 6), dim), (shards_of,), jnp.float32, low / len(shards), largest / len(shards))
        factor_of = factor_of * jnp.repeat(jnp.exp(heights), extent[dim] // shards_of).reshape((-1,) + (1,) * (len(extent) - 1 - dim))
    return factor_of


def centred(stream_key, shape, width, reach, cuts=(), kind=jnp.bfloat16):
    loudness = shard_levels(stream_key, shape, cuts, -0.22, 0.18) if cuts else 1.0
    values = jax.random.normal(stream_key, shape, jnp.float32) * width * loudness
    return jnp.minimum(jnp.maximum(values, -reach), reach).astype(kind)


def setup_inputs(seed: int = 0) -> dict:
    key_list = jax.random.split(jax.random.key(seed), 7)
    return {
        "costs": draw_costs(jax.random.fold_in(key_list[6], 71), 0),
        "block_rows": draw_block_rows(jax.random.fold_in(key_list[6], 71), 0),
        "block_cols": draw_block_cols(jax.random.fold_in(key_list[6], 71), 0),
        "live": draw_live(jax.random.fold_in(key_list[6], 71), 0),
        "log_source": centred(key_list[4], (SRC,), 1.0, 6.0, ((0, 4),), jnp.float32),
        "log_target": centred(key_list[5], (TGT,), 1.0, 6.0, ((0, 8),), jnp.float32),
    }


NEG = -1e30


def reference(costs, block_rows, block_cols, live, log_source, log_target):
    nr, nc, slots, bs, _ = costs.shape
    tiles = costs.reshape(nr * nc * slots, bs, bs)
    dev_r = jnp.broadcast_to(jnp.arange(nr, dtype=jnp.int32)[:, None, None], (nr, nc, slots)).reshape(-1)
    dev_c = jnp.broadcast_to(jnp.arange(nc, dtype=jnp.int32)[None, :, None], (nr, nc, slots)).reshape(-1)
    slot_ids = jnp.broadcast_to(jnp.arange(slots, dtype=jnp.int32)[None, None, :], (nr, nc, slots))
    valid = (slot_ids < live[:, :, None]).reshape(-1)
    row_start = ((dev_r * RB_DEV + block_rows.reshape(-1)) * bs).astype(jnp.int32)
    col_start = ((dev_c * CB_DEV + block_cols.reshape(-1)) * bs).astype(jnp.int32)
    items = (tiles, row_start, col_start, valid)

    def row_lse(target_pot):
        def step(carry, item):
            top, total = carry
            tile, rs, cs, okay = item
            score = lax.dynamic_slice_in_dim(target_pot, cs, bs)[None, :] - tile.astype(jnp.float32)
            old_top = lax.dynamic_slice_in_dim(top, rs, bs)
            old_tot = lax.dynamic_slice_in_dim(total, rs, bs)
            new_top = jnp.maximum(old_top, jnp.max(score, axis=1))
            new_tot = old_tot * jnp.exp(old_top - new_top) + jnp.sum(jnp.exp(score - new_top[:, None]), axis=1)
            new_top = jnp.where(okay, new_top, old_top)
            new_tot = jnp.where(okay, new_tot, old_tot)
            top = lax.dynamic_update_slice_in_dim(top, new_top, rs, 0)
            total = lax.dynamic_update_slice_in_dim(total, new_tot, rs, 0)
            return (top, total), None
        init = (jnp.full((SRC,), NEG, jnp.float32), jnp.zeros((SRC,), jnp.float32))
        (top, total), _ = lax.scan(step, init, items)
        return top + jnp.log(total)

    def col_lse(source_pot):
        def step(carry, item):
            top, total = carry
            tile, rs, cs, okay = item
            score = lax.dynamic_slice_in_dim(source_pot, rs, bs)[:, None] - tile.astype(jnp.float32)
            old_top = lax.dynamic_slice_in_dim(top, cs, bs)
            old_tot = lax.dynamic_slice_in_dim(total, cs, bs)
            new_top = jnp.maximum(old_top, jnp.max(score, axis=0))
            new_tot = old_tot * jnp.exp(old_top - new_top) + jnp.sum(jnp.exp(score - new_top[None, :]), axis=0)
            new_top = jnp.where(okay, new_top, old_top)
            new_tot = jnp.where(okay, new_tot, old_tot)
            top = lax.dynamic_update_slice_in_dim(top, new_top, cs, 0)
            total = lax.dynamic_update_slice_in_dim(total, new_tot, cs, 0)
            return (top, total), None
        init = (jnp.full((TGT,), NEG, jnp.float32), jnp.zeros((TGT,), jnp.float32))
        (top, total), _ = lax.scan(step, init, items)
        return top + jnp.log(total)

    target_pot = jnp.zeros((TGT,), jnp.float32)
    source_pot = jnp.zeros((SRC,), jnp.float32)
    for sweep in range(ITERS):
        source_pot = log_source - row_lse(target_pot)
        target_pot = log_target - col_lse(source_pot)
    return source_pot, target_pot
```

```python
import functools

import jax
import jax.numpy as jnp
from jax import lax
from jax.experimental import pallas as pl
from jax.experimental.pallas import tpu as pltpu
from jax.sharding import PartitionSpec as P

ITERS = 3
NEG = -1e30
LANES = 128
GROUP = 8
MESH = pl.DeviceIdType.MESH


def kernel(
    n_rows, n_cols,
    brows, bcols, live, costs, log_src, log_tgt,
    src_out, tgt_out,
    tiles, tiles_t, rid, cid, slot_top, slot_tot, part_src, src_col, piece, lt_piece,
    cid_all, src_buf, tgt_buf,
    load_sem, cid_send, cid_recv, src_send, src_recv, tgt_send, tgt_recv,
):
    slots, bs, _ = tiles.shape
    halves = bs // LANES
    row_blocks = part_src.shape[0]
    col_blocks = tgt_out.shape[0] // halves
    my_r = lax.axis_index("rows")
    my_c = lax.axis_index("cols")

    barrier = pltpu.get_barrier_semaphore()
    for k in range(1, n_rows):
        pl.semaphore_signal(barrier, inc=1, device_id=(lax.rem(my_r + k, n_rows), my_c), device_id_type=MESH)
    for k in range(1, n_cols):
        pl.semaphore_signal(barrier, inc=1, device_id=(my_r, lax.rem(my_c + k, n_cols)), device_id_type=MESH)

    loads = []
    for c in range(slots // GROUP):
        part = pl.ds(c * GROUP, GROUP)
        loads.append(pltpu.make_async_copy(costs.at[part], tiles.at[part], load_sem.at[c]))
        loads[-1].start()

    count = live[0]
    for t in range(slots):
        okay = t < count
        rid[t : t + 1, :] = jnp.full((1, LANES), jnp.where(okay, brows[t], -1), jnp.int32)
        cid[t : t + 1, :] = jnp.full((1, LANES), jnp.where(okay, bcols[t], -1), jnp.int32)
    wide_cid = cid[...]
    cid_all[pl.ds(my_r, 1)] = wide_cid[None]

    def send(k, along, src, dst, send_sem, recv_sem):
        if along == "rows":
            peer = (lax.rem(my_r + k, n_rows), my_c)
        else:
            peer = (my_r, lax.rem(my_c + k, n_cols))
        return pltpu.make_async_remote_copy(
            src_ref=src, dst_ref=dst, send_sem=send_sem, recv_sem=recv_sem,
            device_id=peer, device_id_type=MESH)

    def exchange(along, n, me, src, buf, send_sem, recv_sem):
        outs = [send(k, along, src, buf.at[me], send_sem.at[k], recv_sem.at[k]) for k in range(1, n)]
        for copy in outs:
            copy.start()
        return outs

    def arrived(along, n, me, src, buf, send_sem, recv_sem):
        for k in range(1, n):
            frm = lax.rem(me + n - k, n)
            send(k, along, src, buf.at[frm], send_sem.at[k], recv_sem.at[k]).wait_recv()

    def group_lse(g, col, tile):
        tops, tots = [], []
        for i in range(GROUP):
            t = g * GROUP + i
            column = col(t, i)
            top_h, tot_h = [], []
            for h in range(halves):
                lanes = slice(h * LANES, (h + 1) * LANES)
                score = -tile(t, lanes) if column is None else column - tile(t, lanes)
                top = jnp.max(score, axis=0, keepdims=True)
                top_h.append(top)
                tot_h.append(jnp.sum(jnp.exp(score - top), axis=0, keepdims=True))
            tops.append(jnp.concatenate(top_h, axis=1))
            tots.append(jnp.concatenate(tot_h, axis=1))
        at = pl.ds(pl.multiple_of(g * GROUP, GROUP), GROUP)
        slot_top[at, :] = jnp.concatenate(tops, axis=0)
        slot_tot[at, :] = jnp.concatenate(tots, axis=0)

    def slot_lse(ids):
        ok = jnp.concatenate([ids] * halves, axis=1) >= 0
        return jnp.where(ok, slot_top[...] + jnp.log(slot_tot[...]), NEG)

    def as_column(row):
        return jnp.concatenate(
            [jnp.broadcast_to(row[:, h * LANES : (h + 1) * LANES], (LANES, LANES)).T for h in range(halves)], axis=0)

    eye = (lax.broadcasted_iota(jnp.int32, (bs, bs), 0) == lax.broadcasted_iota(jnp.int32, (bs, bs), 1))
    eye = eye.astype(jnp.float32).astype(jnp.bfloat16)
    for c in range(slots // GROUP):
        loads[c].wait()

        def turn(t, _):
            tiles_t[t] = lax.dot_general(eye, tiles[t], (((1,), (1,)), ((), ())), preferred_element_type=jnp.float32)
            return 0

        lax.fori_loop(c * GROUP, (c + 1) * GROUP, turn, 0, unroll=2)
        group_lse(c, lambda t, i: None, lambda t, lanes: tiles_t[t, :, lanes])

    pl.semaphore_wait(barrier, n_rows + n_cols - 2)
    cid_copies = exchange("rows", n_rows, my_r, cid, cid_all, cid_send, cid_recv)

    for t in range(slots):
        col_at = bcols[t] * halves
        for h in range(halves):
            lt_piece[t : t + 1, h * LANES : (h + 1) * LANES] = log_tgt[pl.ds(col_at + h, 1), :]
    ls = jnp.concatenate([log_src[pl.ds(h, row_blocks, stride=halves), :] for h in range(halves)], axis=1)

    def wide(mask):
        return jnp.concatenate([mask] * halves, axis=1)

    waits = list(cid_copies)
    block_of = lax.broadcasted_iota(jnp.int32, (row_blocks, LANES), 0)
    for sweep in range(ITERS):
        if sweep:
            def row_group(g, _):
                rows = piece[pl.ds(pl.multiple_of(g * GROUP, GROUP), GROUP), :]
                group_lse(g, lambda t, i: as_column(rows[i : i + 1]), lambda t, lanes: tiles_t[t, :, lanes])
                return 0

            lax.fori_loop(0, slots // GROUP, row_group, 0)
        slot_top[...] = slot_lse(rid[...])
        top = jnp.full((row_blocks, bs), NEG, jnp.float32)
        for t in range(slots):
            here = wide(block_of == rid[t : t + 1, :])
            top = jnp.maximum(top, jnp.where(here, slot_top[t : t + 1, :], NEG))
        total = jnp.zeros((row_blocks, bs), jnp.float32)
        for t in range(slots):
            here = wide(block_of == rid[t : t + 1, :])
            total = total + jnp.exp(jnp.where(here, slot_top[t : t + 1, :], NEG) - top)
        part_src[...] = top + jnp.log(total)
        s_buf = src_buf.at[sweep]
        s_send, s_recv = src_send.at[sweep], src_recv.at[sweep]
        mine = exchange("cols", n_cols, my_c, part_src, s_buf, s_send, s_recv)
        s_buf[pl.ds(my_c, 1)] = part_src[...][None]
        arrived("cols", n_cols, my_c, part_src, s_buf, s_send, s_recv)
        top = s_buf[0]
        for k in range(1, n_cols):
            top = jnp.maximum(top, s_buf[k])
        total = jnp.exp(s_buf[0] - top)
        for k in range(1, n_cols):
            total = total + jnp.exp(s_buf[k] - top)
        source = ls - (top + jnp.log(total))
        for copy in mine:
            copy.wait_send()
        for b in range(row_blocks):
            src_col[b] = as_column(source[b : b + 1, :])

        def col_group(g, _):
            group_lse(g, lambda t, i: src_col[brows[t]], lambda t, lanes: tiles[t, :, lanes].astype(jnp.float32))
            return 0

        lax.fori_loop(0, slots // GROUP, col_group, 0)
        if sweep == 0:
            arrived("rows", n_rows, my_r, cid, cid_all, cid_send, cid_recv)
        t_buf = tgt_buf.at[sweep]
        t_send, t_recv = tgt_send.at[sweep], tgt_recv.at[sweep]
        slot_top[...] = slot_lse(cid[...])
        mine = exchange("rows", n_rows, my_r, slot_top, t_buf, t_send, t_recv)
        t_buf[pl.ds(my_r, 1)] = slot_top[...][None]
        arrived("rows", n_rows, my_r, slot_top, t_buf, t_send, t_recv)
        last = sweep == ITERS - 1
        if last:
            ids = lax.broadcasted_iota(jnp.int32, (col_blocks, LANES), 0)
        else:
            ids = cid[...]

        def gather_lse(ids):
            def each(g):
                at = pl.ds(pl.multiple_of(g * GROUP, GROUP), GROUP)
                for r in range(n_rows):
                    theirs, found = cid_all[r, at, :], t_buf[r, at, :]
                    for i in range(GROUP):
                        here = wide(ids == theirs[i : i + 1])
                        yield jnp.where(here, found[i : i + 1], NEG)

            def top_of(g, top):
                for value in each(g):
                    top = jnp.maximum(top, value)
                return top

            shape = (ids.shape[0], bs)
            top = lax.fori_loop(0, slots // GROUP, top_of, jnp.full(shape, NEG, jnp.float32))

            def total_of(g, total):
                for value in each(g):
                    total = total + jnp.exp(value - top)
                return total

            total = lax.fori_loop(0, slots // GROUP, total_of, jnp.zeros(shape, jnp.float32))
            return top + jnp.log(total)

        if not last:
            piece[...] = jnp.where(wide(ids >= 0), lt_piece[...] - gather_lse(ids), 0.0)
        else:
            per = 16 if col_blocks % 16 == 0 else col_blocks
            for b in range(0, col_blocks, per):
                part = ids[b : b + per]
                found = gather_lse(part)
                for h in range(halves):
                    rows = pl.ds(b * halves + h, per, stride=halves)
                    tgt_out[rows, :] = log_tgt[rows, :] - found[:, h * LANES : (h + 1) * LANES]
            for h in range(halves):
                src_out[pl.ds(h, row_blocks, stride=halves), :] = source[:, h * LANES : (h + 1) * LANES]
        for copy in mine:
            copy.wait_send()
    for copy in waits:
        copy.wait_send()


def per_device(n_rows, n_cols, costs, block_rows, block_cols, live, log_source, log_target):
    tiles = costs[0, 0]
    slots, bs, _ = tiles.shape
    src_rows = log_source.shape[0] // LANES
    tgt_rows = log_target.shape[0] // LANES
    row_blocks = log_source.shape[0] // bs
    f32 = jnp.float32
    dma = pltpu.SemaphoreType.DMA
    smem = pl.BlockSpec(memory_space=pltpu.SMEM)
    vmem = pl.BlockSpec(memory_space=pltpu.VMEM)
    source, target = pl.pallas_call(
        functools.partial(kernel, n_rows, n_cols),
        out_shape=(jax.ShapeDtypeStruct((src_rows, LANES), f32), jax.ShapeDtypeStruct((tgt_rows, LANES), f32)),
        in_specs=[smem, smem, smem, pl.BlockSpec(memory_space=pl.ANY), vmem, vmem],
        out_specs=(vmem, vmem),
        scratch_shapes=[
            pltpu.VMEM((slots, bs, bs), tiles.dtype),
            pltpu.VMEM((slots, bs, bs), f32),
            pltpu.VMEM((slots, LANES), jnp.int32),
            pltpu.VMEM((slots, LANES), jnp.int32),
            pltpu.VMEM((slots, bs), f32),
            pltpu.VMEM((slots, bs), f32),
            pltpu.VMEM((row_blocks, bs), f32),
            pltpu.VMEM((row_blocks, bs, LANES), f32),
            pltpu.VMEM((slots, bs), f32),
            pltpu.VMEM((slots, bs), f32),
            pltpu.VMEM((n_rows, slots, LANES), jnp.int32),
            pltpu.VMEM((ITERS, n_cols, row_blocks, bs), f32),
            pltpu.VMEM((ITERS, n_rows, slots, bs), f32),
            dma((slots // GROUP,)),
            dma((n_rows,)), dma((n_rows,)),
            dma((ITERS, n_cols)), dma((ITERS, n_cols)),
            dma((ITERS, n_rows)), dma((ITERS, n_rows)),
        ],
        compiler_params=pltpu.CompilerParams(collective_id=0, has_side_effects=True),
    )(
        block_rows.reshape(-1), block_cols.reshape(-1), live.reshape(-1), tiles,
        log_source.reshape(src_rows, LANES), log_target.reshape(tgt_rows, LANES),
    )
    return source.reshape(-1), target.reshape(-1)


def solution(mesh):
    in_specs = (
        P("rows", "cols", None, None, None),
        P("rows", "cols", None),
        P("rows", "cols", None),
        P("rows", "cols"),
        P("rows"),
        P("cols"),
    )
    out_specs = (P("rows"), P("cols"))
    body = functools.partial(per_device, mesh.shape["rows"], mesh.shape["cols"])
    return jax.shard_map(body, mesh=mesh, in_specs=in_specs, out_specs=out_specs, check_vma=False)
```

```python
import functools

import jax
import jax.numpy as jnp
from jax import lax
from jax.experimental import pallas as pl
from jax.experimental.pallas import tpu as pltpu
from jax.sharding import PartitionSpec as P

ITERS = 3
NEG = -1e30
LOG2E = 1.4426950408889634
LN2 = 0.6931471805599453
LANES = 128
GROUP = 8
MESH = pl.DeviceIdType.MESH


def log2(x):
    return jnp.log(x) * LOG2E


def kernel(
    n_rows, n_cols,
    brows, bcols, live, costs, log_src, log_tgt,
    src_out, lse_out, ids_out,
    tiles, tiles_s, tiles_t, rid, cid, slot_top, slot_tot, part_src, src_col, piece, lt_piece,
    cid_all, src_buf, tgt_buf,
    load_sem, cid_send, cid_recv, src_send, src_recv, tgt_send, tgt_recv,
):
    slots, bs, _ = tiles.shape
    halves = bs // LANES
    row_blocks = part_src.shape[0]
    my_r = lax.axis_index("rows")
    my_c = lax.axis_index("cols")

    barrier = pltpu.get_barrier_semaphore()
    for k in range(1, n_rows):
        pl.semaphore_signal(barrier, inc=1, device_id=(lax.rem(my_r + k, n_rows), my_c), device_id_type=MESH)
    for k in range(1, n_cols):
        pl.semaphore_signal(barrier, inc=1, device_id=(my_r, lax.rem(my_c + k, n_cols)), device_id_type=MESH)

    loads = []
    for c in range(slots // GROUP):
        part = pl.ds(c * GROUP, GROUP)
        loads.append(pltpu.make_async_copy(costs.at[part], tiles.at[part], load_sem.at[c]))
        loads[-1].start()

    count = live[0]
    for t in range(slots):
        okay = t < count
        rid[t : t + 1, :] = jnp.full((1, LANES), jnp.where(okay, brows[t], -1), jnp.int32)
        cid[t : t + 1, :] = jnp.full((1, LANES), jnp.where(okay, bcols[t], -1), jnp.int32)
    wide_cid = cid[...]
    cid_all[pl.ds(my_r, 1)] = wide_cid[None]

    def send(k, along, src, dst, send_sem, recv_sem):
        if along == "rows":
            peer = (lax.rem(my_r + k, n_rows), my_c)
        else:
            peer = (my_r, lax.rem(my_c + k, n_cols))
        return pltpu.make_async_remote_copy(
            src_ref=src, dst_ref=dst, send_sem=send_sem, recv_sem=recv_sem,
            device_id=peer, device_id_type=MESH)

    def exchange(along, n, me, src, buf, send_sem, recv_sem):
        outs = [send(k, along, src, buf.at[me], send_sem.at[k], recv_sem.at[k]) for k in range(1, n)]
        for copy in outs:
            copy.start()
        return outs

    def arrived(along, n, me, src, buf, send_sem, recv_sem):
        for k in range(1, n):
            frm = lax.rem(me + n - k, n)
            send(k, along, src, buf.at[frm], send_sem.at[k], recv_sem.at[k]).wait_recv()

    def group_lse(g, col, tile):
        tops, tots = [], []
        for i in range(GROUP):
            t = g * GROUP + i
            column = col(t, i)
            top_h, tot_h = [], []
            for h in range(halves):
                lanes = slice(h * LANES, (h + 1) * LANES)
                score = -tile(t, lanes) if column is None else column - tile(t, lanes)
                top = jnp.max(score, axis=0, keepdims=True)
                top_h.append(top)
                tot_h.append(jnp.sum(jnp.exp2(score - top), axis=0, keepdims=True))
            tops.append(jnp.concatenate(top_h, axis=1))
            tots.append(jnp.concatenate(tot_h, axis=1))
        at = pl.ds(pl.multiple_of(g * GROUP, GROUP), GROUP)
        slot_top[at, :] = jnp.concatenate(tops, axis=0)
        slot_tot[at, :] = jnp.concatenate(tots, axis=0)

    def slot_lse(ids):
        ok = jnp.concatenate([ids] * halves, axis=1) >= 0
        return jnp.where(ok, slot_top[...] + log2(slot_tot[...]), NEG)

    def as_column(row):
        return jnp.concatenate(
            [jnp.broadcast_to(row[:, h * LANES : (h + 1) * LANES], (LANES, LANES)).T for h in range(halves)], axis=0)

    eye = (lax.broadcasted_iota(jnp.int32, (bs, bs), 0) == lax.broadcasted_iota(jnp.int32, (bs, bs), 1))
    eye = eye.astype(jnp.float32).astype(jnp.bfloat16)
    for c in range(slots // GROUP):
        loads[c].wait()

        def turn(t, _):
            tile = tiles[t]
            turned = lax.dot_general(eye, tile, (((1,), (1,)), ((), ())), preferred_element_type=jnp.float32)
            tiles_t[t] = turned * LOG2E
            tiles_s[t] = tile.astype(jnp.float32) * LOG2E
            return 0

        lax.fori_loop(c * GROUP, (c + 1) * GROUP, turn, 0, unroll=2)
        group_lse(c, lambda t, i: None, lambda t, lanes: tiles_t[t, :, lanes])

    pl.semaphore_wait(barrier, n_rows + n_cols - 2)
    cid_copies = exchange("rows", n_rows, my_r, cid, cid_all, cid_send, cid_recv)

    for t in range(slots):
        col_at = bcols[t] * halves
        for h in range(halves):
            lt_piece[t : t + 1, h * LANES : (h + 1) * LANES] = log_tgt[pl.ds(col_at + h, 1), :] * LOG2E
    ls = jnp.concatenate([log_src[pl.ds(h, row_blocks, stride=halves), :] * LOG2E for h in range(halves)], axis=1)

    def wide(mask):
        return jnp.concatenate([mask] * halves, axis=1)

    waits = list(cid_copies)
    block_of = lax.broadcasted_iota(jnp.int32, (row_blocks, LANES), 0)
    for sweep in range(ITERS):
        if sweep:
            def row_group(g, _):
                rows = piece[pl.ds(pl.multiple_of(g * GROUP, GROUP), GROUP), :]
                group_lse(g, lambda t, i: as_column(rows[i : i + 1]), lambda t, lanes: tiles_t[t, :, lanes])
                return 0

            lax.fori_loop(0, slots // GROUP, row_group, 0)
        slot_top[...] = slot_lse(rid[...])
        top = jnp.full((row_blocks, bs), NEG, jnp.float32)
        for t in range(slots):
            here = wide(block_of == rid[t : t + 1, :])
            top = jnp.maximum(top, jnp.where(here, slot_top[t : t + 1, :], NEG))
        total = jnp.zeros((row_blocks, bs), jnp.float32)
        for t in range(slots):
            here = wide(block_of == rid[t : t + 1, :])
            total = total + jnp.exp2(jnp.where(here, slot_top[t : t + 1, :], NEG) - top)
        part_src[...] = top + log2(total)
        s_buf = src_buf.at[sweep]
        s_send, s_recv = src_send.at[sweep], src_recv.at[sweep]
        mine = exchange("cols", n_cols, my_c, part_src, s_buf, s_send, s_recv)
        s_buf[pl.ds(my_c, 1)] = part_src[...][None]
        arrived("cols", n_cols, my_c, part_src, s_buf, s_send, s_recv)
        top = s_buf[0]
        for k in range(1, n_cols):
            top = jnp.maximum(top, s_buf[k])
        total = jnp.exp2(s_buf[0] - top)
        for k in range(1, n_cols):
            total = total + jnp.exp2(s_buf[k] - top)
        source = ls - (top + log2(total))
        for copy in mine:
            copy.wait_send()
        for b in range(row_blocks):
            src_col[b] = as_column(source[b : b + 1, :])

        def col_group(g, _):
            group_lse(g, lambda t, i: src_col[brows[t]], lambda t, lanes: tiles_s[t, :, lanes])
            return 0

        lax.fori_loop(0, slots // GROUP, col_group, 0)
        if sweep == 0:
            arrived("rows", n_rows, my_r, cid, cid_all, cid_send, cid_recv)
        t_buf = tgt_buf.at[sweep]
        t_send, t_recv = tgt_send.at[sweep], tgt_recv.at[sweep]
        slot_top[...] = slot_lse(cid[...])
        mine = exchange("rows", n_rows, my_r, slot_top, t_buf, t_send, t_recv)
        t_buf[pl.ds(my_r, 1)] = slot_top[...][None]
        arrived("rows", n_rows, my_r, slot_top, t_buf, t_send, t_recv)
        last = sweep == ITERS - 1

        def gather_lse(ids):
            def each(g):
                at = pl.ds(pl.multiple_of(g * GROUP, GROUP), GROUP)
                for r in range(n_rows):
                    theirs, found = cid_all[r, at, :], t_buf[r, at, :]
                    for i in range(GROUP):
                        here = wide(ids == theirs[i : i + 1])
                        yield jnp.where(here, found[i : i + 1], NEG)

            def top_of(g, top):
                for value in each(g):
                    top = jnp.maximum(top, value)
                return top

            shape = (ids.shape[0], bs)
            top = lax.fori_loop(0, slots // GROUP, top_of, jnp.full(shape, NEG, jnp.float32))

            def total_of(g, total):
                for value in each(g):
                    total = total + jnp.exp2(value - top)
                return total

            total = lax.fori_loop(0, slots // GROUP, total_of, jnp.zeros(shape, jnp.float32))
            return top + log2(total)

        if not last:
            ids = cid[...]
            piece[...] = jnp.where(wide(ids >= 0), lt_piece[...] - gather_lse(ids), 0.0)
        else:
            for r in range(n_rows):
                lse_out[r * slots : (r + 1) * slots, :] = t_buf[r]
                ids_out[r * slots : (r + 1) * slots, :] = cid_all[r]
            src_out[...] = source * LN2
        for copy in mine:
            copy.wait_send()
    for copy in waits:
        copy.wait_send()


def final_kernel(source, lse, ids, log_tgt, src_out, tgt_out, top_buf):
    found, bs = lse.shape
    halves = bs // LANES
    blocks = tgt_out.shape[0] // halves
    exact = functools.partial(jnp.dot, preferred_element_type=jnp.float32, precision=lax.Precision.HIGHEST)
    per = 16 if blocks % 16 == 0 else blocks
    for b in range(0, blocks, per):
        block = lax.broadcasted_iota(jnp.int32, (per, LANES), 0) + b

        def top_of(g, top):
            at = pl.ds(pl.multiple_of(g * GROUP, GROUP), GROUP)
            theirs, values = ids[at, :], lse[at, :]
            for i in range(GROUP):
                here = jnp.concatenate([block == theirs[i : i + 1]] * halves, axis=1)
                top = jnp.maximum(top, jnp.where(here, values[i : i + 1], NEG))
            return top

        top_buf[b : b + per, :] = lax.fori_loop(
            0, found // GROUP, top_of, jnp.full((per, bs), NEG, jnp.float32), unroll=3 if found % (3 * GROUP) == 0 else 2)
    top = top_buf[...]
    names = ids[...].astype(jnp.float32)
    back = (names[:, 0:1] == lax.broadcasted_iota(jnp.int32, (found, blocks), 1).astype(jnp.float32)).astype(jnp.float32)
    into = (names.T[0:1, :] == lax.broadcasted_iota(jnp.int32, (blocks, found), 0).astype(jnp.float32)).astype(jnp.float32)
    total = exact(into, jnp.exp2(lse[...] - exact(back, top)))
    found_lse = top * LN2 + jnp.log(total)
    for h in range(halves):
        rows = pl.ds(h, blocks, stride=halves)
        tgt_out[rows, :] = log_tgt[rows, :] - found_lse[:, h * LANES : (h + 1) * LANES]
        src_out[pl.ds(h, source.shape[0], stride=halves), :] = source[:, h * LANES : (h + 1) * LANES]


def per_device(n_rows, n_cols, costs, block_rows, block_cols, live, log_source, log_target):
    tiles = costs[0, 0]
    slots, bs, _ = tiles.shape
    src_rows = log_source.shape[0] // LANES
    tgt_rows = log_target.shape[0] // LANES
    row_blocks = log_source.shape[0] // bs
    f32 = jnp.float32
    dma = pltpu.SemaphoreType.DMA
    smem = pl.BlockSpec(memory_space=pltpu.SMEM)
    vmem = pl.BlockSpec(memory_space=pltpu.VMEM)
    found = n_rows * slots
    source, lse, ids = pl.pallas_call(
        functools.partial(kernel, n_rows, n_cols),
        out_shape=(
            jax.ShapeDtypeStruct((row_blocks, bs), f32),
            jax.ShapeDtypeStruct((found, bs), f32),
            jax.ShapeDtypeStruct((found, LANES), jnp.int32),
        ),
        in_specs=[smem, smem, smem, pl.BlockSpec(memory_space=pl.ANY), vmem, vmem],
        out_specs=(vmem, vmem, vmem),
        scratch_shapes=[
            pltpu.VMEM((slots, bs, bs), tiles.dtype),
            pltpu.VMEM((slots, bs, bs), f32),
            pltpu.VMEM((slots, bs, bs), f32),
            pltpu.VMEM((slots, LANES), jnp.int32),
            pltpu.VMEM((slots, LANES), jnp.int32),
            pltpu.VMEM((slots, bs), f32),
            pltpu.VMEM((slots, bs), f32),
            pltpu.VMEM((row_blocks, bs), f32),
            pltpu.VMEM((row_blocks, bs, LANES), f32),
            pltpu.VMEM((slots, bs), f32),
            pltpu.VMEM((slots, bs), f32),
            pltpu.VMEM((n_rows, slots, LANES), jnp.int32),
            pltpu.VMEM((ITERS, n_cols, row_blocks, bs), f32),
            pltpu.VMEM((ITERS, n_rows, slots, bs), f32),
            dma((slots // GROUP,)),
            dma((n_rows,)), dma((n_rows,)),
            dma((ITERS, n_cols)), dma((ITERS, n_cols)),
            dma((ITERS, n_rows)), dma((ITERS, n_rows)),
        ],
        compiler_params=pltpu.CompilerParams(collective_id=0, has_side_effects=True, vmem_limit_bytes=62 << 20),
    )(
        block_rows.reshape(-1), block_cols.reshape(-1), live.reshape(-1), tiles,
        log_source.reshape(src_rows, LANES), log_target.reshape(tgt_rows, LANES),
    )
    source, target = pl.pallas_call(
        final_kernel,
        out_shape=(jax.ShapeDtypeStruct((src_rows, LANES), f32), jax.ShapeDtypeStruct((tgt_rows, LANES), f32)),
        in_specs=[vmem] * 4,
        out_specs=(vmem, vmem),
        scratch_shapes=[pltpu.VMEM((tgt_rows * LANES // bs, bs), f32)],
        compiler_params=pltpu.CompilerParams(vmem_limit_bytes=8 << 20),
    )(source, lse, ids, log_target.reshape(tgt_rows, LANES))
    return source.reshape(-1), target.reshape(-1)


def solution(mesh):
    in_specs = (
        P("rows", "cols", None, None, None),
        P("rows", "cols", None),
        P("rows", "cols", None),
        P("rows", "cols"),
        P("rows"),
        P("cols"),
    )
    out_specs = (P("rows"), P("cols"))
    body = functools.partial(per_device, mesh.shape["rows"], mesh.shape["cols"])
    return jax.shard_map(body, mesh=mesh, in_specs=in_specs, out_specs=out_specs, check_vma=False)
```

```python
import functools

import jax
import jax.numpy as jnp
from jax import lax
from jax.experimental import pallas as pl
from jax.experimental.pallas import tpu as pltpu
from jax.sharding import PartitionSpec as P

ITERS = 3
NEG = -1e30
LOG2E = 1.4426950408889634
LN2 = 0.6931471805599453
LANES = 128
GROUP = 8
MESH = pl.DeviceIdType.MESH


def log2(x):
    return jnp.log(x) * LOG2E


def kernel(
    n_rows, n_cols,
    brows, bcols, live, costs, log_src, log_tgt,
    src_out, lse_out, ids_out,
    tiles, tiles_s, tiles_t, rid, cid, slot_top, slot_tot, part_src, part_tgt, columns, src_col, piece, lt_piece,
    cid_all, src_buf, tgt_buf,
    load_sem, cid_send, cid_recv, src_send, src_recv, tgt_send, tgt_recv,
):
    slots, bs, _ = tiles.shape
    halves = bs // LANES
    row_blocks = part_src.shape[1]
    my_r = lax.axis_index("rows")
    my_c = lax.axis_index("cols")

    barrier = pltpu.get_barrier_semaphore()
    for k in range(1, n_rows):
        pl.semaphore_signal(barrier, inc=1, device_id=(lax.rem(my_r + k, n_rows), my_c), device_id_type=MESH)
    for k in range(1, n_cols):
        pl.semaphore_signal(barrier, inc=1, device_id=(my_r, lax.rem(my_c + k, n_cols)), device_id_type=MESH)

    loads = []
    for c in range(slots // GROUP):
        part = pl.ds(c * GROUP, GROUP)
        loads.append(pltpu.make_async_copy(costs.at[part], tiles.at[part], load_sem.at[c]))
        loads[-1].start()

    count = live[0]
    for t in range(slots):
        okay = t < count
        rid[t : t + 1, :] = jnp.full((1, LANES), jnp.where(okay, brows[t], -1), jnp.int32)
        cid[t : t + 1, :] = jnp.full((1, LANES), jnp.where(okay, bcols[t], -1), jnp.int32)
    wide_cid = cid[...]
    cid_all[pl.ds(my_r, 1)] = wide_cid[None]

    def send(k, along, src, dst, send_sem, recv_sem):
        if along == "rows":
            peer = (lax.rem(my_r + k, n_rows), my_c)
        else:
            peer = (my_r, lax.rem(my_c + k, n_cols))
        return pltpu.make_async_remote_copy(
            src_ref=src, dst_ref=dst, send_sem=send_sem, recv_sem=recv_sem,
            device_id=peer, device_id_type=MESH)

    def exchange(along, n, me, src, buf, send_sem, recv_sem):
        outs = [send(k, along, src, buf.at[me], send_sem.at[k], recv_sem.at[k]) for k in range(1, n)]
        for copy in outs:
            copy.start()
        return outs

    def arrived(along, n, me, src, buf, send_sem, recv_sem):
        for k in range(1, n):
            frm = lax.rem(me + n - k, n)
            send(k, along, src, buf.at[frm], send_sem.at[k], recv_sem.at[k]).wait_recv()

    def group_lse(g, h, col, tile):
        lanes = slice(h * LANES, (h + 1) * LANES)
        tops, tots = [], []
        for i in range(GROUP):
            t = g * GROUP + i
            column = col(t, i)
            score = -tile[t, :, lanes] if column is None else column - tile[t, :, lanes]
            top = jnp.max(score, axis=0, keepdims=True)
            tops.append(top)
            tots.append(jnp.sum(jnp.exp2(score - top), axis=0, keepdims=True))
        at = pl.ds(pl.multiple_of(g * GROUP, GROUP), GROUP)
        slot_top[h, at, :] = jnp.concatenate(tops, axis=0)
        slot_tot[h, at, :] = jnp.concatenate(tots, axis=0)

    def slot_lse(h, ids):
        return jnp.where(ids >= 0, slot_top[h] + log2(slot_tot[h]), NEG)

    def as_column(row):
        return jnp.concatenate(
            [jnp.broadcast_to(row[:, h * LANES : (h + 1) * LANES], (LANES, LANES)).T for h in range(halves)], axis=0)

    eye = (lax.broadcasted_iota(jnp.int32, (bs, bs), 0) == lax.broadcasted_iota(jnp.int32, (bs, bs), 1))
    eye = eye.astype(jnp.float32).astype(jnp.bfloat16)
    for c in range(slots // GROUP):
        loads[c].wait()

        def turn(t, _):
            tile = tiles[t]
            turned = lax.dot_general(eye, tile, (((1,), (1,)), ((), ())), preferred_element_type=jnp.float32)
            tiles_t[t] = turned * LOG2E
            tiles_s[t] = tile.astype(jnp.float32) * LOG2E
            return 0

        lax.fori_loop(c * GROUP, (c + 1) * GROUP, turn, 0, unroll=2)
        for h in range(halves):
            group_lse(c, h, lambda t, i: None, tiles_t)

    pl.semaphore_wait(barrier, n_rows + n_cols - 2)
    cid_copies = exchange("rows", n_rows, my_r, cid, cid_all, cid_send, cid_recv)

    for t in range(slots):
        col_at = bcols[t] * halves
        for h in range(halves):
            lt_piece[h, t : t + 1, :] = log_tgt[pl.ds(col_at + h, 1), :] * LOG2E
    waits = list(cid_copies)
    block_of = lax.broadcasted_iota(jnp.int32, (row_blocks, LANES), 0)
    for sweep in range(ITERS):
        mine = []
        for h in range(halves):
            if sweep:
                def row_group(g, _):
                    at = pl.ds(pl.multiple_of(g * GROUP, GROUP), GROUP)
                    rows = jnp.concatenate([piece[k, at, :] for k in range(halves)], axis=1)

                    def column(t, i):
                        if h:
                            return columns[t]
                        made = as_column(rows[i : i + 1])
                        columns[t] = made
                        return made

                    group_lse(g, h, column, tiles_t)
                    return 0

                lax.fori_loop(0, slots // GROUP, row_group, 0)
            found = slot_lse(h, rid[...])
            masked = [jnp.where(block_of == rid[t : t + 1, :], found[t : t + 1, :], NEG) for t in range(slots)]
            top = functools.reduce(jnp.maximum, masked)
            total = functools.reduce(jnp.add, [jnp.exp2(value - top) for value in masked])
            part_src[h] = top + log2(total)
            mine += exchange("cols", n_cols, my_c, part_src.at[h], src_buf.at[sweep, h], src_send.at[sweep, h], src_recv.at[sweep, h])
            src_buf[sweep, h, pl.ds(my_c, 1)] = part_src[h][None]
        sources = []
        for h in range(halves):
            arrived("cols", n_cols, my_c, part_src.at[h], src_buf.at[sweep, h], src_send.at[sweep, h], src_recv.at[sweep, h])
            theirs = [src_buf[sweep, h, k] for k in range(n_cols)]
            top = functools.reduce(jnp.maximum, theirs)
            total = functools.reduce(jnp.add, [jnp.exp2(value - top) for value in theirs])
            source = log_src[pl.ds(h, row_blocks, stride=halves), :] * LOG2E - (top + log2(total))
            sources.append(source)
            for b in range(row_blocks):
                src_col[b, h * LANES : (h + 1) * LANES, :] = jnp.broadcast_to(source[b : b + 1, :], (LANES, LANES)).T
        for copy in mine:
            copy.wait_send()
        if sweep == 0:
            arrived("rows", n_rows, my_r, cid, cid_all, cid_send, cid_recv)
        mine = []
        for h in range(halves):
            def col_group(g, _):
                group_lse(g, h, lambda t, i: src_col[brows[t]], tiles_s)
                return 0

            lax.fori_loop(0, slots // GROUP, col_group, 0)
            part_tgt[h] = slot_lse(h, cid[...])
            mine += exchange("rows", n_rows, my_r, part_tgt.at[h], tgt_buf.at[sweep, h], tgt_send.at[sweep, h], tgt_recv.at[sweep, h])
            tgt_buf[sweep, h, pl.ds(my_r, 1)] = part_tgt[h][None]
        for h in range(halves):
            arrived("rows", n_rows, my_r, part_tgt.at[h], tgt_buf.at[sweep, h], tgt_send.at[sweep, h], tgt_recv.at[sweep, h])
            lanes = slice(h * LANES, (h + 1) * LANES)
            if sweep == ITERS - 1:
                for r in range(n_rows):
                    lse_out[r * slots : (r + 1) * slots, lanes] = tgt_buf[sweep, h, r]
                    ids_out[r * slots : (r + 1) * slots, :] = cid_all[r]
                src_out[:, lanes] = sources[h] * LN2
                continue
            ids = cid[...]

            def each(g):
                at = pl.ds(pl.multiple_of(g * GROUP, GROUP), GROUP)
                for r in range(n_rows):
                    theirs, values = cid_all[r, at, :], tgt_buf[sweep, h, r, at, :]
                    for i in range(GROUP):
                        yield jnp.where(ids == theirs[i : i + 1], values[i : i + 1], NEG)

            def top_of(g, top):
                return functools.reduce(jnp.maximum, each(g), top)

            top = lax.fori_loop(0, slots // GROUP, top_of, jnp.full(ids.shape, NEG, jnp.float32))

            def total_of(g, total):
                return functools.reduce(lambda so_far, value: so_far + jnp.exp2(value - top), each(g), total)

            total = lax.fori_loop(0, slots // GROUP, total_of, jnp.zeros(ids.shape, jnp.float32))
            piece[h] = jnp.where(ids >= 0, lt_piece[h] - (top + log2(total)), 0.0)
        for copy in mine:
            copy.wait_send()
    for copy in waits:
        copy.wait_send()


def final_kernel(source, lse, ids, log_tgt, src_out, tgt_out, top_buf):
    found, bs = lse.shape
    halves = bs // LANES
    blocks = tgt_out.shape[0] // halves
    exact = functools.partial(jnp.dot, preferred_element_type=jnp.float32, precision=lax.Precision.HIGHEST)
    per = 16 if blocks % 16 == 0 else blocks
    for b in range(0, blocks, per):
        block = lax.broadcasted_iota(jnp.int32, (per, LANES), 0) + b

        def top_of(g, top):
            at = pl.ds(pl.multiple_of(g * GROUP, GROUP), GROUP)
            theirs, values = ids[at, :], lse[at, :]
            for i in range(GROUP):
                here = jnp.concatenate([block == theirs[i : i + 1]] * halves, axis=1)
                top = jnp.maximum(top, jnp.where(here, values[i : i + 1], NEG))
            return top

        top_buf[b : b + per, :] = lax.fori_loop(
            0, found // GROUP, top_of, jnp.full((per, bs), NEG, jnp.float32), unroll=3 if found % (3 * GROUP) == 0 else 2)
    top = top_buf[...]
    names = ids[...].astype(jnp.float32)
    back = (names[:, 0:1] == lax.broadcasted_iota(jnp.int32, (found, blocks), 1).astype(jnp.float32)).astype(jnp.float32)
    into = (names.T[0:1, :] == lax.broadcasted_iota(jnp.int32, (blocks, found), 0).astype(jnp.float32)).astype(jnp.float32)
    total = exact(into, jnp.exp2(lse[...] - exact(back, top)))
    found_lse = top * LN2 + jnp.log(total)
    for h in range(halves):
        rows = pl.ds(h, blocks, stride=halves)
        tgt_out[rows, :] = log_tgt[rows, :] - found_lse[:, h * LANES : (h + 1) * LANES]
        src_out[pl.ds(h, source.shape[0], stride=halves), :] = source[:, h * LANES : (h + 1) * LANES]


def per_device(n_rows, n_cols, costs, block_rows, block_cols, live, log_source, log_target):
    tiles = costs[0, 0]
    slots, bs, _ = tiles.shape
    src_rows = log_source.shape[0] // LANES
    tgt_rows = log_target.shape[0] // LANES
    row_blocks = log_source.shape[0] // bs
    f32 = jnp.float32
    halves = bs // LANES
    dma = pltpu.SemaphoreType.DMA
    smem = pl.BlockSpec(memory_space=pltpu.SMEM)
    vmem = pl.BlockSpec(memory_space=pltpu.VMEM)
    found = n_rows * slots
    source, lse, ids = pl.pallas_call(
        functools.partial(kernel, n_rows, n_cols),
        out_shape=(
            jax.ShapeDtypeStruct((row_blocks, bs), f32),
            jax.ShapeDtypeStruct((found, bs), f32),
            jax.ShapeDtypeStruct((found, LANES), jnp.int32),
        ),
        in_specs=[smem, smem, smem, pl.BlockSpec(memory_space=pl.ANY), vmem, vmem],
        out_specs=(vmem, vmem, vmem),
        scratch_shapes=[
            pltpu.VMEM((slots, bs, bs), tiles.dtype),
            pltpu.VMEM((slots, bs, bs), f32),
            pltpu.VMEM((slots, bs, bs), f32),
            pltpu.VMEM((slots, LANES), jnp.int32),
            pltpu.VMEM((slots, LANES), jnp.int32),
            pltpu.VMEM((halves, slots, LANES), f32),
            pltpu.VMEM((halves, slots, LANES), f32),
            pltpu.VMEM((halves, row_blocks, LANES), f32),
            pltpu.VMEM((halves, slots, LANES), f32),
            pltpu.VMEM((slots, bs, LANES), f32),
            pltpu.VMEM((row_blocks, bs, LANES), f32),
            pltpu.VMEM((halves, slots, LANES), f32),
            pltpu.VMEM((halves, slots, LANES), f32),
            pltpu.VMEM((n_rows, slots, LANES), jnp.int32),
            pltpu.VMEM((ITERS, halves, n_cols, row_blocks, LANES), f32),
            pltpu.VMEM((ITERS, halves, n_rows, slots, LANES), f32),
            dma((slots // GROUP,)),
            dma((n_rows,)), dma((n_rows,)),
            dma((ITERS, halves, n_cols)), dma((ITERS, halves, n_cols)),
            dma((ITERS, halves, n_rows)), dma((ITERS, halves, n_rows)),
        ],
        compiler_params=pltpu.CompilerParams(collective_id=0, has_side_effects=True),
    )(
        block_rows.reshape(-1), block_cols.reshape(-1), live.reshape(-1), tiles,
        log_source.reshape(src_rows, LANES), log_target.reshape(tgt_rows, LANES),
    )
    source, target = pl.pallas_call(
        final_kernel,
        out_shape=(jax.ShapeDtypeStruct((src_rows, LANES), f32), jax.ShapeDtypeStruct((tgt_rows, LANES), f32)),
        in_specs=[vmem] * 4,
        out_specs=(vmem, vmem),
        scratch_shapes=[pltpu.VMEM((tgt_rows * LANES // bs, bs), f32)],
    )(source, lse, ids, log_target.reshape(tgt_rows, LANES))
    return source.reshape(-1), target.reshape(-1)


def solution(mesh):
    in_specs = (
        P("rows", "cols", None, None, None),
        P("rows", "cols", None),
        P("rows", "cols", None),
        P("rows", "cols"),
        P("rows"),
        P("cols"),
    )
    out_specs = (P("rows"), P("cols"))
    body = functools.partial(per_device, mesh.shape["rows"], mesh.shape["cols"])
    return jax.shard_map(body, mesh=mesh, in_specs=in_specs, out_specs=out_specs, check_vma=False)
```
